128 devices in a mesh: dp: 8 (over z, core), mp: 16 (over y, x).
Axes of the slice: x: 4, y: 4, z: 4, core: 2. Of those that a mesh axis runs over, the one named last changes fastest.
Arguments:
- acts: bfloat16 [1024, 8192], P('dp', 'mp'), may hold values from -6 to 6
- w_up: bfloat16 [8192, 14336], P(None, 'mp'), may hold values from -0.0625 to 0.0625
- out_grad: bfloat16 [1024, 14336], P('dp', 'mp'), may hold values from -6 to 6
- rotation: float32 [8192, 8192], P('mp', 'dp'), may hold values from -6 to 6
Outputs:
- half_rotation: float32 [8192, 8192], P('mp', 'dp')
- next_rotation: float32 [8192, 8192], P('mp', 'dp')
The draws below stay inside these ranges and needn't reach their ends.
All inputs are finite; a program needn't handle non-finite values.
Results may differ from the reference program's by a relative error of at most 0.017.
Values may be sent and summed in bfloat16 or wider, within the bound.
A program may use at most 128 MiB of HBM per device.

```python
import math
import jax
import jax.numpy as jnp
from jax import lax

D = 8192
FW = 14336
TOK_DEV = 128
ITERS = 2
TOKENS = 1024
N_DP = 8
N_MP = 16


def block_levels(rng, dims, pieces, low, top_value):
    loudness, own = 1.0, jax.random.fold_in(rng, 6)
    for dim, shards_of in pieces:
        draws = jnp.exp(jax.random.uniform(jax.random.fold_in(own, dim), (shards_of,), jnp.float32, low / len(pieces), top_value / len(pieces)))
        loudness = loudness * jnp.repeat(draws, dims[dim] // shards_of).reshape([-1 if axis == dim else 1 for axis in range(len(dims))])
    return loudness


def noise(key, dims, scale, limit, pieces=(), held_as=jnp.bfloat16):
    values = scale * jax.random.normal(key, dims, jnp.float32)
    if pieces:
        values = values * block_levels(key, dims, pieces, -0.22, 0.18)
    return jnp.clip(values, -limit, limit).astype(held_as)


def setup_inputs(seed: int = 0) -> dict:
    seeds = jax.random.split(jax.random.key(seed), 5)
    acts = noise(seeds[0], (TOKENS, D), 1.0, 6.0, ((0, 8), (1, 16)))
    w_up = noise(seeds[1], (D, FW), D ** -0.5, 0.0625, ((1, 16),))
    out_grad = noise(seeds[2], (TOKENS, FW), 1.0, 6.0, ((0, 8), (1, 16)))
    rotation = noise(seeds[3], (D, D), 1.0, 6.0, ((0, 16), (1, 8)), jnp.float32)
    return dict(acts=acts, w_up=w_up, out_grad=out_grad, rotation=rotation)


step_gain = 0.5
epsilon = 1e-06

def settle(term):
    return lax.optimization_barrier(term.astype(jnp.bfloat16)).astype(jnp.float32)

def block_sum(left, right, blocks, factor_scale):
    width = left.shape[1] // blocks
    total = jnp.zeros((left.shape[0], right.shape[1]), jnp.float32)
    for block in range(blocks):
        term = jnp.dot(left[:, block * width:(block + 1) * width], right[block * width:(block + 1) * width, :], preferred_element_type=jnp.float32)
        total = total + settle(term * factor_scale)
    return total

def reference(acts, w_up, out_grad, rotation):
    inv_root = D ** (-0.5)
    rot_half = rotation.astype(jnp.bfloat16)
    mixed = block_sum(acts, rot_half, N_MP, inv_root).astype(jnp.bfloat16)
    hidden = jnp.dot(mixed, w_up, preferred_element_type=jnp.float32)
    sigmoid_hidden = jax.nn.sigmoid(hidden)
    grad_hidden = (out_grad.astype(jnp.float32) * sigmoid_hidden * (1.0 + hidden * (1.0 - sigmoid_hidden))).astype(jnp.bfloat16)
    grad_mixed = block_sum(grad_hidden, w_up.T, N_MP, 1.0).astype(jnp.bfloat16)
    factor = jnp.dot(grad_mixed, rot_half.T, preferred_element_type=jnp.float32).astype(jnp.bfloat16)
    act_norm = jnp.sum(jnp.square(acts.astype(jnp.float32)))
    factor_norm = jnp.sum(jnp.square(factor.astype(jnp.float32)))
    spread = (TOKENS ** (-0.5) + D ** (-0.5)) ** 2
    step_size = step_gain * math.sqrt(D) / (jnp.sqrt((act_norm + epsilon) * (factor_norm + epsilon)) * spread)
    current = rotation
    first_iterate = rotation
    for iteration in range(ITERS):
        point = (rotation + current).astype(jnp.bfloat16)
        left = block_sum(factor, point, N_MP, inv_root).astype(jnp.bfloat16)
        right = block_sum(acts, point, N_MP, inv_root).astype(jnp.bfloat16)
        update = jnp.zeros((D, D), jnp.float32)
        for group in range(N_DP):
            first = group * TOK_DEV
            last = first + TOK_DEV
            term = jnp.dot(acts[first:last].T, left[first:last], preferred_element_type=jnp.float32) - jnp.dot(factor[first:last].T, right[first:last], preferred_element_type=jnp.float32)
            update = update + settle(term)
        current = rotation - step_size * update
        if iteration == 0:
            first_iterate = current
    return (first_iterate, current)
```

```python
import math

import jax
import jax.numpy as jnp
from jax import lax
from jax.sharding import PartitionSpec as P

D = 8192
step_gain = 0.5
epsilon = 1e-06


def contract_cols(left, right):
    return lax.dot_general(
        left, right, (((1,), (1,)), ((), ())), preferred_element_type=jnp.float32
    )


def contract_rows(left, right):
    return lax.dot_general(
        left, right, (((0,), (0,)), ((), ())), preferred_element_type=jnp.float32
    )


def local(acts, w_up, out_grad, rotation):
    inv_root = D ** (-0.5)
    rows = acts.shape[0]
    me = lax.axis_index("dp")
    tokens = rows * lax.axis_size("dp")
    rot_half = rotation.astype(jnp.bfloat16)
    rot_rows = lax.all_gather(rot_half, "dp", axis=1, tiled=True)
    acts_all = lax.all_gather(acts, "dp", axis=0, tiled=True)
    mixed = lax.psum(
        (jnp.dot(acts, rot_rows, preferred_element_type=jnp.float32) * inv_root).astype(
            jnp.bfloat16
        ),
        "mp",
    )
    hidden = jnp.dot(mixed, w_up, preferred_element_type=jnp.float32)
    sigmoid_hidden = jax.nn.sigmoid(hidden)
    grad_hidden = (
        out_grad.astype(jnp.float32) * sigmoid_hidden * (1.0 + hidden * (1.0 - sigmoid_hidden))
    ).astype(jnp.bfloat16)
    grad_mixed = lax.psum(contract_cols(grad_hidden, w_up).astype(jnp.bfloat16), "mp")
    right = 2 * lax.all_to_all(mixed, "dp", split_axis=1, concat_axis=0, tiled=True)
    factor = contract_cols(grad_mixed, rot_rows).astype(jnp.bfloat16)
    factor_all = lax.all_gather(factor, "dp", axis=0, tiled=True)
    spread_rows = jnp.concatenate((factor_all, acts_all), axis=0)
    skew_rows = jnp.concatenate((acts_all, -factor_all), axis=0)
    own = jnp.concatenate((acts, -factor), axis=0)
    left = lax.psum(
        (jnp.dot(factor_all, rot_half, preferred_element_type=jnp.float32) * (2 * inv_root)).astype(
            jnp.bfloat16
        ),
        "mp",
    )
    gram = lax.psum(contract_cols(spread_rows, own).astype(jnp.bfloat16), "mp")
    second = contract_rows(skew_rows, gram).astype(jnp.bfloat16)
    eye = jnp.eye(rows, dtype=jnp.float32)
    act_sq = lax.dynamic_slice(gram, (tokens + me * rows, 0), (rows, rows))
    factor_sq = lax.dynamic_slice(gram, (me * rows, rows), (rows, rows))
    squares = jnp.concatenate(
        (jnp.sum(act_sq * eye, axis=0), jnp.sum(factor_sq * -eye, axis=0))
    ).astype(jnp.bfloat16)
    packed = jnp.concatenate((second, jnp.broadcast_to(squares, (16, 2 * rows))), axis=0)
    gathered = lax.all_gather(packed, "dp", axis=0)
    width = second.shape[0]
    parts = gathered[:, width].astype(jnp.float32)
    act_norm = jnp.sum(parts[:, :rows])
    factor_norm = jnp.sum(parts[:, rows:])
    second_all = (
        gathered[:, :width].reshape(-1, width, 2, rows).transpose(1, 2, 0, 3).reshape(width, -1)
    )
    spread = (tokens ** (-0.5) + D ** (-0.5)) ** 2
    step_size = (
        step_gain
        * math.sqrt(D)
        / (jnp.sqrt((act_norm + epsilon) * (factor_norm + epsilon)) * spread)
    )
    first_map = skew_rows.T
    second_map = (
        first_map.astype(jnp.float32) - (step_size * inv_root) * second_all.astype(jnp.float32)
    ).astype(jnp.bfloat16)
    sides = jnp.concatenate((left, right), axis=0)
    half = rotation - step_size * jnp.dot(first_map, sides, preferred_element_type=jnp.float32)
    full = rotation - step_size * jnp.dot(second_map, sides, preferred_element_type=jnp.float32)
    return half, full


def solution(mesh):
    placed = (P("dp", "mp"), P(None, "mp"), P("dp", "mp"), P("mp", "dp"))
    return jax.shard_map(
        local,
        mesh=mesh,
        in_specs=placed,
        out_specs=(P("mp", "dp"), P("mp", "dp")),
        check_vma=False,
    )
```

```python
import functools
import math

import jax
import jax.numpy as jnp
from jax import lax
from jax.experimental import pallas as pl
from jax.experimental.pallas import tpu as pltpu
from jax.sharding import PartitionSpec as P

D = 8192
step_gain = 0.5
epsilon = 1e-06


MESH = pl.DeviceIdType.MESH
N_DP = 8
SIDE = 4


def cut(ref, dim, start, size, lead=()):
    if dim == 1:
        return ref.at[(*lead, slice(None), pl.ds(start, size))]
    return ref.at[(*lead, pl.ds(start, size), slice(None))]


def kernel(dims, modes, *refs):
    n, e = len(dims), len(modes)
    xs, ys = refs[:n], refs[n : n + e]
    sums, outs = refs[n + e : 2 * n + e], refs[2 * n + e : 2 * (n + e)]
    scratch = refs[2 * (n + e) :]
    first, held, second = scratch[:n], scratch[n : 2 * n], scratch[2 * n : 3 * n]
    send, recv, dp_send, dp_recv, local_sem = scratch[3 * n :]
    dp, mp = lax.axis_index("dp"), lax.axis_index("mp")
    at = (mp // SIDE, mp % SIDE)

    def peer(axis, k):
        j = (at[axis] + k) % SIDE
        return j, (dp, j * SIDE + at[1] if axis == 0 else at[0] * SIDE + j)

    barrier = pltpu.get_barrier_semaphore()
    greeted = 0
    if n:
        for axis in (0, 1):
            for k in range(1, SIDE):
                pl.semaphore_signal(barrier, inc=1, device_id=peer(axis, k)[1], device_id_type=MESH)
                greeted += 1
    if e:
        for k in range(1, N_DP):
            pl.semaphore_signal(
                barrier, inc=1, device_id=((dp + k) % N_DP, mp), device_id_type=MESH
            )
            greeted += 1
    pl.semaphore_wait(barrier, greeted)

    started = []

    def send_to(src, dst, index, device):
        copy = pltpu.make_async_remote_copy(
            src_ref=src,
            dst_ref=dst,
            send_sem=send.at[index],
            recv_sem=recv.at[index],
            device_id=device,
            device_id_type=MESH,
        )
        copy.start()
        started.append(copy)
        return copy

    todo = [(h, a) for h in range(2) for a in range(n)]
    flight = {}

    def spot(a, h):
        size = xs[a].shape[dims[a]]
        p, q = (1, 0) if h == 0 else (0, 1)
        return p, q, h * (size // 2), size // 8, size // 32

    def index(stage, h, a, k):
        return ((stage * 2 + h) * n + a) * 3 + k - 1

    order = (2, 1, 3)
    for h, a in todo:
        p, q, base, big, small = spot(a, h)
        copies = []
        for k in order:
            j, device = peer(p, k)
            start = pl.multiple_of(base + j * big, big)
            copies.append(
                send_to(
                    cut(xs[a], dims[a], start, big),
                    first[a].at[h, k - 1],
                    index(0, h, a, k),
                    device,
                )
            )
        flight[0, h, a] = copies
    exchanges = []
    for i, mode in enumerate(modes):
        rows = ys[i].shape[0]
        here = pl.multiple_of(dp * rows, rows)
        width = outs[i].shape[1]

        def part(to):
            if mode == "gather":
                return ys[i]
            return ys[i].at[:, pl.ds(pl.multiple_of(to * width, width), width)]

        own = pltpu.make_async_copy(part(dp), outs[i].at[pl.ds(here, rows), :], local_sem.at[i])
        own.start()
        exchanges.append(own)
        for k in (4, 3, 5, 2, 6, 1, 7):
            to = (dp + k) % N_DP
            copy = pltpu.make_async_remote_copy(
                src_ref=part(to),
                dst_ref=outs[i].at[pl.ds(here, rows), :],
                send_sem=dp_send.at[i * 7 + k - 1],
                recv_sem=dp_recv.at[i * 7 + k - 1],
                device_id=(to, mp),
                device_id_type=MESH,
            )
            copy.start()
            exchanges.append(copy)
    for h, a in todo:
        p, q, base, big, small = spot(a, h)
        for copy in flight[0, h, a]:
            copy.wait_recv()
        start = pl.multiple_of(base + at[p] * big, big)
        total = cut(xs[a], dims[a], start, big)[...].astype(jnp.float32)
        for k in range(3):
            total += first[a][h, k].astype(jnp.float32)
        held[a][h] = total.astype(jnp.bfloat16)
        copies = []
        for k in order:
            j, device = peer(q, k)
            copies.append(
                send_to(
                    cut(held[a], dims[a], pl.multiple_of(j * small, small), small, (h,)),
                    second[a].at[h, k - 1],
                    index(1, h, a, k),
                    device,
                )
            )
        flight[1, h, a] = copies
    for h, a in todo:
        p, q, base, big, small = spot(a, h)
        for copy in flight[1, h, a]:
            copy.wait_recv()
        total = cut(held[a], dims[a], pl.multiple_of(at[q] * small, small), small, (h,))[
            ...
        ].astype(jnp.float32)
        for k in range(3):
            total += second[a][h, k].astype(jnp.float32)
        block = cut(
            sums[a], dims[a], pl.multiple_of(base + at[p] * big + at[q] * small, small), small
        )
        block[...] = total.astype(jnp.bfloat16)
        flight[2, h, a] = [
            send_to(block, block, index(2, h, a, k), peer(q, k)[1]) for k in order
        ]
    for h, a in todo:
        p, q, base, big, small = spot(a, h)
        for copy in flight[2, h, a]:
            copy.wait_recv()
        block = cut(sums[a], dims[a], pl.multiple_of(base + at[p] * big, big), big)
        flight[3, h, a] = [
            send_to(block, block, index(3, h, a, k), peer(p, k)[1]) for k in order
        ]
    for h, a in todo:
        for copy in flight[3, h, a]:
            copy.wait_recv()
    for copy in started:
        copy.wait_send()
    for copy in exchanges:
        copy.wait()


def communicate(number, name, adds=(), moves=()):
    dims = [dim for _, dim in adds]
    modes = [mode for _, mode in moves]
    arrays = [x for x, _ in adds] + [y for y, _ in moves]
    shapes = [x.shape for x, _ in adds]
    for y, mode in moves:
        width = y.shape[1] if mode == "gather" else y.shape[1] // N_DP
        shapes.append((y.shape[0] * N_DP, width))

    def piece(x, dim, parts):
        shape = list(x.shape)
        shape[dim] //= parts
        return tuple(shape)

    first = [pltpu.VMEM((2, 3, *piece(x, d, 8)), jnp.bfloat16) for x, d in adds]
    held = [pltpu.VMEM((2, *piece(x, d, 8)), jnp.bfloat16) for x, d in adds]
    second = [pltpu.VMEM((2, 3, *piece(x, d, 32)), jnp.bfloat16) for x, d in adds]
    dma = pltpu.SemaphoreType.DMA
    return pl.pallas_call(
        functools.partial(kernel, dims, modes),
        out_shape=[jax.ShapeDtypeStruct(s, jnp.bfloat16) for s in shapes],
        in_specs=[pl.BlockSpec(memory_space=pltpu.VMEM)] * len(arrays),
        out_specs=[pl.BlockSpec(memory_space=pltpu.VMEM)] * len(arrays),
        scratch_shapes=[
            *first,
            *held,
            *second,
            dma((max(24 * len(adds), 1),)),
            dma((max(24 * len(adds), 1),)),
            dma((max(7 * len(moves), 1),)),
            dma((max(7 * len(moves), 1),)),
            dma((max(len(moves), 1),)),
        ],
        compiler_params=pltpu.CompilerParams(
            collective_id=number, has_side_effects=True, vmem_limit_bytes=32 * 1024 * 1024
        ),
        name=name,
    )(*arrays)


def contract_cols(left, right):
    return lax.dot_general(
        left, right, (((1,), (1,)), ((), ())), preferred_element_type=jnp.float32
    )


def contract_rows(left, right):
    return lax.dot_general(
        left, right, (((0,), (0,)), ((), ())), preferred_element_type=jnp.float32
    )


def local(acts, w_up, out_grad, rotation):
    inv_root = D ** (-0.5)
    rows = acts.shape[0]
    me = lax.axis_index("dp")
    tokens = rows * lax.axis_size("dp")
    rot_half = rotation.astype(jnp.bfloat16)
    rot_rows = lax.all_gather(rot_half, "dp", axis=1, tiled=True)
    mixed_part = (jnp.dot(acts, rot_rows, preferred_element_type=jnp.float32) * inv_root).astype(
        jnp.bfloat16
    )
    mixed, acts_all = communicate(0, "sum_mixed", [(mixed_part, 1)], [(acts, "gather")])
    hidden = jnp.dot(mixed, w_up, preferred_element_type=jnp.float32)
    sigmoid_hidden = jax.nn.sigmoid(hidden)
    grad_hidden = (
        out_grad.astype(jnp.float32) * sigmoid_hidden * (1.0 + hidden * (1.0 - sigmoid_hidden))
    ).astype(jnp.bfloat16)
    grad_part = contract_cols(grad_hidden, w_up).astype(jnp.bfloat16)
    grad_mixed, right = communicate(1, "sum_grad", [(grad_part, 1)], [(mixed, "transpose")])
    right = 2 * right
    factor = contract_cols(grad_mixed, rot_rows).astype(jnp.bfloat16)
    (factor_all,) = communicate(2, "gather_factor", [], [(factor, "gather")])
    spread_rows = jnp.concatenate((factor_all, acts_all), axis=0)
    skew_rows = jnp.concatenate((acts_all, -factor_all), axis=0)
    own = jnp.concatenate((acts, -factor), axis=0)
    left_part = (
        jnp.dot(factor_all, rot_half, preferred_element_type=jnp.float32) * (2 * inv_root)
    ).astype(jnp.bfloat16)
    gram_part = contract_cols(spread_rows, own).astype(jnp.bfloat16)
    (gram,) = communicate(3, "sum_gram", [(gram_part, 0)], [])
    second = contract_rows(skew_rows, gram).astype(jnp.bfloat16)
    eye = jnp.eye(rows, dtype=jnp.float32)
    act_sq = lax.dynamic_slice(gram, (tokens + me * rows, 0), (rows, rows))
    factor_sq = lax.dynamic_slice(gram, (me * rows, rows), (rows, rows))
    squares = jnp.concatenate(
        (jnp.sum(act_sq * eye, axis=0), jnp.sum(factor_sq * -eye, axis=0))
    ).astype(jnp.bfloat16)
    packed = jnp.concatenate((second, jnp.broadcast_to(squares, (16, 2 * rows))), axis=0)
    left, gathered = communicate(4, "sum_left", [(left_part, 0)], [(packed, "gather")])
    gathered = gathered.reshape(-1, *packed.shape)
    width = second.shape[0]
    parts = gathered[:, width].astype(jnp.float32)
    act_norm = jnp.sum(parts[:, :rows])
    factor_norm = jnp.sum(parts[:, rows:])
    second_all = (
        gathered[:, :width].reshape(-1, width, 2, rows).transpose(1, 2, 0, 3).reshape(width, -1)
    )
    spread = (tokens ** (-0.5) + D ** (-0.5)) ** 2
    step_size = (
        step_gain
        * math.sqrt(D)
        / (jnp.sqrt((act_norm + epsilon) * (factor_norm + epsilon)) * spread)
    )
    first_map = skew_rows.T
    second_map = (
        first_map.astype(jnp.float32) - (step_size * inv_root) * second_all.astype(jnp.float32)
    ).astype(jnp.bfloat16)
    sides = jnp.concatenate((left, right), axis=0)
    half = rotation - step_size * jnp.dot(first_map, sides, preferred_element_type=jnp.float32)
    full = rotation - step_size * jnp.dot(second_map, sides, preferred_element_type=jnp.float32)
    return half, full


def solution(mesh):
    placed = (P("dp", "mp"), P(None, "mp"), P("dp", "mp"), P("mp", "dp"))
    return jax.shard_map(
        local,
        mesh=mesh,
        in_specs=placed,
        out_specs=(P("mp", "dp"), P("mp", "dp")),
        check_vma=False,
    )
```

```python
import functools
import math

import jax
import jax.numpy as jnp
from jax import lax
from jax.experimental import pallas as pl
from jax.experimental.pallas import tpu as pltpu
from jax.sharding import PartitionSpec as P

D = 8192
step_gain = 0.5
epsilon = 1e-06


MESH = pl.DeviceIdType.MESH
N_DP = 8
SIDE = 4


def cut(ref, dim, start, size, lead=()):
    if dim == 1:
        return ref.at[(*lead, slice(None), pl.ds(start, size))]
    return ref.at[(*lead, pl.ds(start, size), slice(None))]


def kernel(dims, arrays, modes, *refs):
    n, e = len(dims), arrays
    xs, ys = refs[:n], refs[n : n + e]
    sums, outs = refs[n + e : 2 * n + e], refs[2 * n + e : 2 * (n + e)]
    scratch = refs[2 * (n + e) :]
    first, held, second = scratch[:n], scratch[n : 2 * n], scratch[2 * n : 3 * n]
    send, recv, dp_send, dp_recv, local_sem = scratch[3 * n :]
    dp, mp = lax.axis_index("dp"), lax.axis_index("mp")
    at = (mp // SIDE, mp % SIDE)

    def peer(axis, k):
        j = (at[axis] + k) % SIDE
        return j, (dp, j * SIDE + at[1] if axis == 0 else at[0] * SIDE + j)

    barrier = pltpu.get_barrier_semaphore()
    greeted = 0
    if n:
        for axis in (0, 1):
            for k in range(1, SIDE):
                pl.semaphore_signal(barrier, inc=1, device_id=peer(axis, k)[1], device_id_type=MESH)
                greeted += 1
    if e:
        for k in range(1, N_DP):
            pl.semaphore_signal(
                barrier, inc=1, device_id=((dp + k) % N_DP, mp), device_id_type=MESH
            )
            greeted += 1
    pl.semaphore_wait(barrier, greeted)

    started = []

    def send_to(src, dst, index, device):
        copy = pltpu.make_async_remote_copy(
            src_ref=src,
            dst_ref=dst,
            send_sem=send.at[index],
            recv_sem=recv.at[index],
            device_id=device,
            device_id_type=MESH,
        )
        copy.start()
        started.append(copy)
        return copy

    todo = [(h, a) for h in range(2) for a in range(n)]
    flight = {}

    def spot(a, h):
        size = xs[a].shape[dims[a]]
        p, q = (1, 0) if h == 0 else (0, 1)
        return p, q, h * (size // 2), size // 8, size // 32

    def index(stage, h, a, k):
        return ((stage * 2 + h) * n + a) * 3 + k - 1

    order = (2, 1, 3)
    for h, a in todo:
        p, q, base, big, small = spot(a, h)
        copies = []
        for k in order:
            j, device = peer(p, k)
            start = pl.multiple_of(base + j * big, big)
            copies.append(
                send_to(
                    cut(xs[a], dims[a], start, big),
                    first[a].at[h, k - 1],
                    index(0, h, a, k),
                    device,
                )
            )
        flight[0, h, a] = copies
    exchanges = []
    for i, mode in enumerate(modes):
        which, block, blocks, split = mode
        rows = ys[which].shape[0] // blocks
        here = pl.ds(pl.multiple_of((block * N_DP + dp) * rows, rows), rows)
        width = outs[which].shape[1]

        def part(to):
            if not split:
                return ys[which].at[pl.ds(block * rows, rows), :]
            return ys[which].at[:, pl.ds(pl.multiple_of(to * width, width), width)]

        landing = outs[which].at[here, :]
        own = pltpu.make_async_copy(part(dp), landing, local_sem.at[i])
        own.start()
        exchanges.append(own)
        for k in (4, 3, 5, 2, 6, 1, 7):
            to = (dp + k) % N_DP
            copy = pltpu.make_async_remote_copy(
                src_ref=part(to),
                dst_ref=landing,
                send_sem=dp_send.at[i * 7 + k - 1],
                recv_sem=dp_recv.at[i * 7 + k - 1],
                device_id=(to, mp),
                device_id_type=MESH,
            )
            copy.start()
            exchanges.append(copy)
    for h, a in todo:
        p, q, base, big, small = spot(a, h)
        for copy in flight[0, h, a]:
            copy.wait_recv()
        start = pl.multiple_of(base + at[p] * big, big)
        total = cut(xs[a], dims[a], start, big)[...].astype(jnp.float32)
        for k in range(3):
            total += first[a][h, k].astype(jnp.float32)
        held[a][h] = total.astype(jnp.bfloat16)
        copies = []
        for k in order:
            j, device = peer(q, k)
            copies.append(
                send_to(
                    cut(held[a], dims[a], pl.multiple_of(j * small, small), small, (h,)),
                    second[a].at[h, k - 1],
                    index(1, h, a, k),
                    device,
                )
            )
        flight[1, h, a] = copies
    for h, a in todo:
        p, q, base, big, small = spot(a, h)
        for copy in flight[1, h, a]:
            copy.wait_recv()
        total = cut(held[a], dims[a], pl.multiple_of(at[q] * small, small), small, (h,))[
            ...
        ].astype(jnp.float32)
        for k in range(3):
            total += second[a][h, k].astype(jnp.float32)
        block = cut(
            sums[a], dims[a], pl.multiple_of(base + at[p] * big + at[q] * small, small), small
        )
        block[...] = total.astype(jnp.bfloat16)
        flight[2, h, a] = [
            send_to(block, block, index(2, h, a, k), peer(q, k)[1]) for k in order
        ]
    for h, a in todo:
        p, q, base, big, small = spot(a, h)
        for copy in flight[2, h, a]:
            copy.wait_recv()
        block = cut(sums[a], dims[a], pl.multiple_of(base + at[p] * big, big), big)
        flight[3, h, a] = [
            send_to(block, block, index(3, h, a, k), peer(p, k)[1]) for k in order
        ]
    for h, a in todo:
        for copy in flight[3, h, a]:
            copy.wait_recv()
    for copy in started:
        copy.wait_send()
    for copy in exchanges:
        copy.wait()


def communicate(number, name, adds=(), moves=()):
    dims = [dim for _, dim in adds]
    modes = []
    for i, (_, mode) in enumerate(moves):
        if mode == "transpose":
            modes.append((i, 0, 1, True))
        else:
            modes.extend((i, s, mode, False) for s in range(mode))
    arrays = [x for x, _ in adds] + [y for y, _ in moves]
    shapes = [x.shape for x, _ in adds]
    for y, mode in moves:
        width = y.shape[1] // N_DP if mode == "transpose" else y.shape[1]
        shapes.append((y.shape[0] * N_DP, width))

    def piece(x, dim, parts):
        shape = list(x.shape)
        shape[dim] //= parts
        return tuple(shape)

    first = [pltpu.VMEM((2, 3, *piece(x, d, 8)), jnp.bfloat16) for x, d in adds]
    held = [pltpu.VMEM((2, *piece(x, d, 8)), jnp.bfloat16) for x, d in adds]
    second = [pltpu.VMEM((2, 3, *piece(x, d, 32)), jnp.bfloat16) for x, d in adds]
    dma = pltpu.SemaphoreType.DMA
    return pl.pallas_call(
        functools.partial(kernel, dims, len(moves), modes),
        out_shape=[jax.ShapeDtypeStruct(s, jnp.bfloat16) for s in shapes],
        in_specs=[pl.BlockSpec(memory_space=pltpu.VMEM)] * len(arrays),
        out_specs=[pl.BlockSpec(memory_space=pltpu.VMEM)] * len(arrays),
        scratch_shapes=[
            *first,
            *held,
            *second,
            dma((max(24 * len(adds), 1),)),
            dma((max(24 * len(adds), 1),)),
            dma((max(7 * len(modes), 1),)),
            dma((max(7 * len(modes), 1),)),
            dma((max(len(modes), 1),)),
        ],
        compiler_params=pltpu.CompilerParams(
            collective_id=number, has_side_effects=True, vmem_limit_bytes=32 * 1024 * 1024
        ),
        name=name,
    )(*arrays)


def contract_cols(left, right):
    return lax.dot_general(
        left, right, (((1,), (1,)), ((), ())), preferred_element_type=jnp.float32
    )


def contract_rows(left, right):
    return lax.dot_general(
        left, right, (((0,), (0,)), ((), ())), preferred_element_type=jnp.float32
    )


def local(acts, w_up, out_grad, rotation):
    inv_root = D ** (-0.5)
    rows = acts.shape[0]
    me = lax.axis_index("dp")
    tokens = rows * lax.axis_size("dp")
    rot_half = rotation.astype(jnp.bfloat16)
    rot_rows = lax.all_gather(rot_half, "dp", axis=1, tiled=True)
    mixed_part = (jnp.dot(acts, rot_rows, preferred_element_type=jnp.float32) * inv_root).astype(
        jnp.bfloat16
    )
    mixed, acts_all = communicate(0, "sum_mixed", [(mixed_part, 1)], [(acts, 1)])
    hidden = jnp.dot(mixed, w_up, preferred_element_type=jnp.float32)
    sigmoid_hidden = jax.nn.sigmoid(hidden)
    grad_hidden = (
        out_grad.astype(jnp.float32) * sigmoid_hidden * (1.0 + hidden * (1.0 - sigmoid_hidden))
    ).astype(jnp.bfloat16)
    grad_part = contract_cols(grad_hidden, w_up).astype(jnp.bfloat16)
    grad_mixed, right = communicate(1, "sum_grad", [(grad_part, 1)], [(mixed, "transpose")])
    right = 2 * right
    factor = contract_cols(grad_mixed, rot_rows).astype(jnp.bfloat16)
    (factor_all,) = communicate(2, "gather_factor", [], [(factor, 1)])
    spread_rows = jnp.concatenate((factor_all, acts_all), axis=0)
    skew_rows = jnp.concatenate((acts_all, -factor_all), axis=0)
    own = jnp.concatenate((acts, -factor), axis=0)
    left_part = (
        jnp.dot(factor_all, rot_half, preferred_element_type=jnp.float32) * (2 * inv_root)
    ).astype(jnp.bfloat16)
    gram_part = contract_cols(spread_rows, own).astype(jnp.bfloat16)
    (gram,) = communicate(3, "sum_gram", [(gram_part, 0)], [])
    second = contract_rows(gram, skew_rows).astype(jnp.bfloat16)
    eye = jnp.eye(rows, dtype=jnp.float32)
    act_sq = lax.dynamic_slice(gram, (tokens + me * rows, 0), (rows, rows))
    factor_sq = lax.dynamic_slice(gram, (me * rows, rows), (rows, rows))
    squares = jnp.concatenate(
        (jnp.sum(act_sq * eye, axis=0), jnp.sum(factor_sq * -eye, axis=0))
    ).astype(jnp.bfloat16)
    squares = jnp.broadcast_to(squares, (16, 2 * rows))
    left, second_all, parts = communicate(
        4, "sum_left", [(left_part, 0)], [(second, 2), (squares, 1)]
    )
    parts = parts[::16].astype(jnp.float32)
    act_norm = jnp.sum(parts[:, :rows])
    factor_norm = jnp.sum(parts[:, rows:])
    spread = (tokens ** (-0.5) + D ** (-0.5)) ** 2
    step_size = (
        step_gain
        * math.sqrt(D)
        / (jnp.sqrt((act_norm + epsilon) * (factor_norm + epsilon)) * spread)
    )
    second_map = (
        skew_rows.astype(jnp.float32) - (step_size * inv_root) * second_all.astype(jnp.float32)
    ).astype(jnp.bfloat16)
    sides = jnp.concatenate((left, right), axis=0)
    half = rotation - step_size * contract_rows(skew_rows, sides)
    full = rotation - step_size * contract_rows(second_map, sides)
    return half, full


def solution(mesh):
    placed = (P("dp", "mp"), P(None, "mp"), P("dp", "mp"), P("mp", "dp"))
    return jax.shard_map(
        local,
        mesh=mesh,
        in_specs=placed,
        out_specs=(P("mp", "dp"), P("mp", "dp")),
        check_vma=False,
    )
```

```python
import functools
import math

import jax
import jax.numpy as jnp
from jax import lax
from jax.experimental import pallas as pl
from jax.experimental.pallas import tpu as pltpu
from jax.sharding import PartitionSpec as P

D = 8192
step_gain = 0.5
epsilon = 1e-06


MESH = pl.DeviceIdType.MESH
N_DP = 8
SIDE = 4


def cut(ref, dim, start, size, lead=()):
    if dim == 1:
        return ref.at[(*lead, slice(None), pl.ds(start, size))]
    return ref.at[(*lead, pl.ds(start, size), slice(None))]


def kernel(dims, arrays, modes, *refs):
    n, e = len(dims), arrays
    xs, ys = refs[:n], refs[n : n + e]
    sums, outs = refs[n + e : 2 * n + e], refs[2 * n + e : 2 * (n + e)]
    scratch = refs[2 * (n + e) :]
    first, held, second = scratch[:n], scratch[n : 2 * n], scratch[2 * n : 3 * n]
    send, recv, dp_send, dp_recv, local_sem = scratch[3 * n :]
    dp, mp = lax.axis_index("dp"), lax.axis_index("mp")
    at = (mp // SIDE, mp % SIDE)

    def peer(axis, k):
        j = (at[axis] + k) % SIDE
        return j, (dp, j * SIDE + at[1] if axis == 0 else at[0] * SIDE + j)

    barrier = pltpu.get_barrier_semaphore()
    greeted = 0
    if n:
        for axis in (0, 1):
            for k in range(1, SIDE):
                pl.semaphore_signal(barrier, inc=1, device_id=peer(axis, k)[1], device_id_type=MESH)
                greeted += 1
    if e:
        for k in range(1, N_DP):
            pl.semaphore_signal(
                barrier, inc=1, device_id=((dp + k) % N_DP, mp), device_id_type=MESH
            )
            greeted += 1
    pl.semaphore_wait(barrier, greeted)

    started = []

    def send_to(src, dst, index, device):
        copy = pltpu.make_async_remote_copy(
            src_ref=src,
            dst_ref=dst,
            send_sem=send.at[index],
            recv_sem=recv.at[index],
            device_id=device,
            device_id_type=MESH,
        )
        copy.start()
        started.append(copy)
        return copy

    todo = [(h, a) for h in range(2) for a in range(n)]
    flight = {}

    def spot(a, h):
        size = xs[a].shape[dims[a]]
        p, q = (1, 0) if h == 0 else (0, 1)
        return p, q, h * (size // 2), size // 8, size // 32

    def index(stage, h, a, k):
        return ((stage * 2 + h) * n + a) * 3 + k - 1

    order = (2, 1, 3)
    for h, a in todo:
        p, q, base, big, small = spot(a, h)
        copies = []
        for k in order:
            j, device = peer(p, k)
            start = pl.multiple_of(base + j * big, big)
            copies.append(
                send_to(
                    cut(xs[a], dims[a], start, big),
                    first[a].at[h, k - 1],
                    index(0, h, a, k),
                    device,
                )
            )
        flight[0, h, a] = copies
    exchanges = []
    for i, mode in enumerate(modes):
        which, block, blocks, split = mode
        rows = ys[which].shape[0] // blocks
        here = pl.ds(pl.multiple_of((block * N_DP + dp) * rows, rows), rows)
        width = outs[which].shape[1]

        def part(to):
            if not split:
                return ys[which].at[pl.ds(block * rows, rows), :]
            return ys[which].at[:, pl.ds(pl.multiple_of(to * width, width), width)]

        landing = outs[which].at[here, :]
        own = pltpu.make_async_copy(part(dp), landing, local_sem.at[i])
        own.start()
        exchanges.append(own)
        for k in (4, 3, 5, 2, 6, 1, 7):
            to = (dp + k) % N_DP
            copy = pltpu.make_async_remote_copy(
                src_ref=part(to),
                dst_ref=landing,
                send_sem=dp_send.at[i * 7 + k - 1],
                recv_sem=dp_recv.at[i * 7 + k - 1],
                device_id=(to, mp),
                device_id_type=MESH,
            )
            copy.start()
            exchanges.append(copy)
    for h, a in todo:
        p, q, base, big, small = spot(a, h)
        for copy in flight[0, h, a]:
            copy.wait_recv()
        start = pl.multiple_of(base + at[p] * big, big)
        total = cut(xs[a], dims[a], start, big)[...].astype(jnp.float32)
        for k in range(3):
            total += first[a][h, k].astype(jnp.float32)
        held[a][h] = total.astype(jnp.bfloat16)
        copies = []
        for k in order:
            j, device = peer(q, k)
            copies.append(
                send_to(
                    cut(held[a], dims[a], pl.multiple_of(j * small, small), small, (h,)),
                    second[a].at[h, k - 1],
                    index(1, h, a, k),
                    device,
                )
            )
        flight[1, h, a] = copies
    for h, a in todo:
        p, q, base, big, small = spot(a, h)
        for copy in flight[1, h, a]:
            copy.wait_recv()
        total = cut(held[a], dims[a], pl.multiple_of(at[q] * small, small), small, (h,))[
            ...
        ].astype(jnp.float32)
        for k in range(3):
            total += second[a][h, k].astype(jnp.float32)
        block = cut(
            sums[a], dims[a], pl.multiple_of(base + at[p] * big + at[q] * small, small), small
        )
        block[...] = total.astype(jnp.bfloat16)
        flight[2, h, a] = [
            send_to(block, block, index(2, h, a, k), peer(q, k)[1]) for k in order
        ]
    for h, a in todo:
        p, q, base, big, small = spot(a, h)
        for copy in flight[2, h, a]:
            copy.wait_recv()
        block = cut(sums[a], dims[a], pl.multiple_of(base + at[p] * big, big), big)
        flight[3, h, a] = [
            send_to(block, block, index(3, h, a, k), peer(p, k)[1]) for k in order
        ]
    for h, a in todo:
        for copy in flight[3, h, a]:
            copy.wait_recv()
    for copy in started:
        copy.wait_send()
    for copy in exchanges:
        copy.wait()


def communicate(number, name, adds=(), moves=()):
    dims = [dim for _, dim in adds]
    modes = []
    for i, (_, mode) in enumerate(moves):
        if mode == "transpose":
            modes.append((i, 0, 1, True))
        else:
            modes.extend((i, s, mode, False) for s in range(mode))
    arrays = [x for x, _ in adds] + [y for y, _ in moves]
    shapes = [x.shape for x, _ in adds]
    for y, mode in moves:
        width = y.shape[1] // N_DP if mode == "transpose" else y.shape[1]
        shapes.append((y.shape[0] * N_DP, width))

    def piece(x, dim, parts):
        shape = list(x.shape)
        shape[dim] //= parts
        return tuple(shape)

    first = [pltpu.VMEM((2, 3, *piece(x, d, 8)), jnp.bfloat16) for x, d in adds]
    held = [pltpu.VMEM((2, *piece(x, d, 8)), jnp.bfloat16) for x, d in adds]
    second = [pltpu.VMEM((2, 3, *piece(x, d, 32)), jnp.bfloat16) for x, d in adds]
    dma = pltpu.SemaphoreType.DMA
    return pl.pallas_call(
        functools.partial(kernel, dims, len(moves), modes),
        out_shape=[jax.ShapeDtypeStruct(s, jnp.bfloat16) for s in shapes],
        in_specs=[pl.BlockSpec(memory_space=pltpu.VMEM)] * len(arrays),
        out_specs=[pl.BlockSpec(memory_space=pltpu.VMEM)] * len(arrays),
        scratch_shapes=[
            *first,
            *held,
            *second,
            dma((max(24 * len(adds), 1),)),
            dma((max(24 * len(adds), 1),)),
            dma((max(7 * len(modes), 1),)),
            dma((max(7 * len(modes), 1),)),
            dma((max(len(modes), 1),)),
        ],
        compiler_params=pltpu.CompilerParams(
            collective_id=number, has_side_effects=True, vmem_limit_bytes=32 * 1024 * 1024
        ),
        name=name,
    )(*arrays)


def mix_kernel(x, out, first, held, second, piece, send, recv, dp_send, dp_recv, local_sem):
    dp, mp = lax.axis_index("dp"), lax.axis_index("mp")
    at = (mp // SIDE, mp % SIDE)
    rows, half = x.shape[0], x.shape[1] // 2
    big, small = rows // 4, rows // 16
    few = small // N_DP
    wide = out.shape[1] // 2

    def peer(axis, k):
        j = (at[axis] + k) % SIDE
        return j, (dp, j * SIDE + at[1] if axis == 0 else at[0] * SIDE + j)

    barrier = pltpu.get_barrier_semaphore()
    for axis in (0, 1):
        for k in range(1, SIDE):
            pl.semaphore_signal(barrier, inc=1, device_id=peer(axis, k)[1], device_id_type=MESH)
    for k in range(1, N_DP):
        pl.semaphore_signal(barrier, inc=1, device_id=((dp + k) % N_DP, mp), device_id_type=MESH)
    pl.semaphore_wait(barrier, 2 * (SIDE - 1) + N_DP - 1)

    started = []

    def send_to(src, dst, sems, index, device):
        copy = pltpu.make_async_remote_copy(
            src_ref=src,
            dst_ref=dst,
            send_sem=sems[0].at[index],
            recv_sem=sems[1].at[index],
            device_id=device,
            device_id_type=MESH,
        )
        copy.start()
        started.append(copy)
        return copy

    over_mp, over_dp = (send, recv), (dp_send, dp_recv)
    order = (2, 1, 3)
    axes = ((1, 0), (0, 1))
    flight = {}

    def index(stage, h, k):
        return (stage * 2 + h) * 3 + k - 1

    for h in range(2):
        p, q = axes[h]
        copies = []
        for k in order:
            j, device = peer(p, k)
            src = x.at[pl.ds(pl.multiple_of(j * big, big), big), pl.ds(h * half, half)]
            copies.append(send_to(src, first.at[h, k - 1], over_mp, index(0, h, k), device))
        flight[0, h] = copies
    for h in range(2):
        p, q = axes[h]
        for copy in flight[0, h]:
            copy.wait_recv()
        total = x[pl.ds(pl.multiple_of(at[p] * big, big), big), pl.ds(h * half, half)].astype(
            jnp.float32
        )
        for k in range(3):
            total += first[h, k].astype(jnp.float32)
        held[h] = total.astype(jnp.bfloat16)
        copies = []
        for k in order:
            j, device = peer(q, k)
            src = held.at[h, pl.ds(pl.multiple_of(j * small, small), small), :]
            copies.append(send_to(src, second.at[h, k - 1], over_mp, index(1, h, k), device))
        flight[1, h] = copies
    for h in range(2):
        p, q = axes[h]
        for copy in flight[1, h]:
            copy.wait_recv()
        total = held[h, pl.ds(pl.multiple_of(at[q] * small, small), small), :].astype(jnp.float32)
        for k in range(3):
            total += second[h, k].astype(jnp.float32)
        piece[h] = total.astype(jnp.bfloat16)
        tokens = pl.ds(pl.multiple_of((at[p] * SIDE + at[q]) * few, few), few)
        landing = out.at[tokens, pl.ds(pl.multiple_of(h * wide + dp * half, half), half)]
        own = pltpu.make_async_copy(
            piece.at[h, pl.ds(pl.multiple_of(dp * few, few), few), :], landing, local_sem.at[h]
        )
        own.start()
        copies = []
        for k in (4, 3, 5, 2, 6, 1, 7):
            to = (dp + k) % N_DP
            src = piece.at[h, pl.ds(pl.multiple_of(to * few, few), few), :]
            copies.append(send_to(src, landing, over_dp, h * 7 + k - 1, (to, mp)))
        flight[2, h] = (own, copies)
    for h in range(2):
        p, q = axes[h]
        own, copies = flight[2, h]
        own.wait()
        for copy in copies:
            copy.wait_recv()
        tokens = pl.ds(pl.multiple_of((at[p] * SIDE + at[q]) * few, few), few)
        block = out.at[tokens, pl.ds(h * wide, wide)]
        flight[3, h] = [
            send_to(block, block, over_mp, index(2, h, k), peer(q, k)[1]) for k in order
        ]
    for h in range(2):
        p, q = axes[h]
        for copy in flight[3, h]:
            copy.wait_recv()
        tokens = pl.ds(pl.multiple_of(at[p] * SIDE * few, SIDE * few), SIDE * few)
        block = out.at[tokens, pl.ds(h * wide, wide)]
        flight[4, h] = [
            send_to(block, block, over_mp, index(3, h, k), peer(p, k)[1]) for k in order
        ]
    for h in range(2):
        for copy in flight[4, h]:
            copy.wait_recv()
    for copy in started:
        copy.wait_send()


def mix(x):
    rows, columns = x.shape
    dma = pltpu.SemaphoreType.DMA
    half = columns // 2
    return pl.pallas_call(
        mix_kernel,
        out_shape=jax.ShapeDtypeStruct((rows // N_DP, columns * N_DP), jnp.bfloat16),
        in_specs=[pl.BlockSpec(memory_space=pltpu.VMEM)],
        out_specs=pl.BlockSpec(memory_space=pltpu.VMEM),
        scratch_shapes=[
            pltpu.VMEM((2, 3, rows // 4, half), jnp.bfloat16),
            pltpu.VMEM((2, rows // 4, half), jnp.bfloat16),
            pltpu.VMEM((2, 3, rows // 16, half), jnp.bfloat16),
            pltpu.VMEM((2, rows // 16, half), jnp.bfloat16),
            dma((24,)),
            dma((24,)),
            dma((14,)),
            dma((14,)),
            dma((2,)),
        ],
        compiler_params=pltpu.CompilerParams(
            collective_id=0, has_side_effects=True, vmem_limit_bytes=32 * 1024 * 1024
        ),
        name="sum_mixed",
    )(x)


def contract_cols(left, right):
    return lax.dot_general(
        left, right, (((1,), (1,)), ((), ())), preferred_element_type=jnp.float32
    )


def contract_rows(left, right):
    return lax.dot_general(
        left, right, (((0,), (0,)), ((), ())), preferred_element_type=jnp.float32
    )


def local(acts, w_up, out_grad, rotation):
    inv_root = D ** (-0.5)
    rows = acts.shape[0]
    me = lax.axis_index("dp")
    tokens = rows * lax.axis_size("dp")
    rot_half = rotation.astype(jnp.bfloat16)
    rot_rows = lax.all_gather(rot_half, "dp", axis=1, tiled=True)
    (acts_all,) = communicate(5, "gather_acts", [], [(acts, 1)])
    blocks = SIDE * SIDE
    by_block = acts_all.reshape(-1, blocks, rows // blocks, acts.shape[1])
    by_block = by_block.transpose(1, 0, 2, 3).reshape(acts_all.shape)
    mixed_part = (
        jnp.dot(by_block, rot_half, preferred_element_type=jnp.float32) * inv_root
    ).astype(jnp.bfloat16)
    mixed = mix(mixed_part)
    run = mixed.shape[1] // (2 * N_DP)
    starts = [(h * N_DP + d) * run for d in range(N_DP) for h in range(2)]
    mixed = jnp.concatenate([mixed[:, start : start + run] for start in starts], axis=1)
    hidden = jnp.dot(mixed, w_up, preferred_element_type=jnp.float32)
    sigmoid_hidden = jax.nn.sigmoid(hidden)
    grad_hidden = (
        out_grad.astype(jnp.float32) * sigmoid_hidden * (1.0 + hidden * (1.0 - sigmoid_hidden))
    ).astype(jnp.bfloat16)
    grad_part = contract_cols(grad_hidden, w_up).astype(jnp.bfloat16)
    grad_mixed, right = communicate(1, "sum_grad", [(grad_part, 1)], [(mixed, "transpose")])
    right = 2 * right
    factor = contract_cols(grad_mixed, rot_rows).astype(jnp.bfloat16)
    (factor_all,) = communicate(2, "gather_factor", [], [(factor, 1)])
    spread_rows = jnp.concatenate((factor_all, acts_all), axis=0)
    skew_rows = jnp.concatenate((acts_all, -factor_all), axis=0)
    own = jnp.concatenate((acts, -factor), axis=0)
    left_part = (
        jnp.dot(factor_all, rot_half, preferred_element_type=jnp.float32) * (2 * inv_root)
    ).astype(jnp.bfloat16)
    gram_part = contract_cols(spread_rows, own).astype(jnp.bfloat16)
    (gram,) = communicate(3, "sum_gram", [(gram_part, 0)], [])
    second = contract_rows(gram, skew_rows).astype(jnp.bfloat16)
    eye = jnp.eye(rows, dtype=jnp.float32)
    act_sq = lax.dynamic_slice(gram, (tokens + me * rows, 0), (rows, rows))
    factor_sq = lax.dynamic_slice(gram, (me * rows, rows), (rows, rows))
    squares = jnp.concatenate(
        (jnp.sum(act_sq * eye, axis=0), jnp.sum(factor_sq * -eye, axis=0))
    ).astype(jnp.bfloat16)
    squares = jnp.broadcast_to(squares, (16, 2 * rows))
    left, second_all, parts = communicate(
        4, "sum_left", [(left_part, 0)], [(second, 2), (squares, 1)]
    )
    parts = parts[::16].astype(jnp.float32)
    act_norm = jnp.sum(parts[:, :rows])
    factor_norm = jnp.sum(parts[:, rows:])
    spread = (tokens ** (-0.5) + D ** (-0.5)) ** 2
    step_size = (
        step_gain
        * math.sqrt(D)
        / (jnp.sqrt((act_norm + epsilon) * (factor_norm + epsilon)) * spread)
    )
    second_map = (
        skew_rows.astype(jnp.float32) - (step_size * inv_root) * second_all.astype(jnp.float32)
    ).astype(jnp.bfloat16)
    sides = jnp.concatenate((left, right), axis=0)
    half = rotation - step_size * contract_rows(skew_rows, sides)
    full = rotation - step_size * contract_rows(second_map, sides)
    return half, full


def solution(mesh):
    placed = (P("dp", "mp"), P(None, "mp"), P("dp", "mp"), P("mp", "dp"))
    return jax.shard_map(
        local,
        mesh=mesh,
        in_specs=placed,
        out_specs=(P("mp", "dp"), P("mp", "dp")),
        check_vma=False,
    )
```

```python
import functools
import math

import jax
import jax.numpy as jnp
from jax import lax
from jax.experimental import pallas as pl
from jax.experimental.pallas import tpu as pltpu
from jax.sharding import PartitionSpec as P

D = 8192
step_gain = 0.5
epsilon = 1e-06


MESH = pl.DeviceIdType.MESH
N_DP = 8
SIDE = 4


def cut(ref, dim, start, size, lead=()):
    if dim == 1:
        return ref.at[(*lead, slice(None), pl.ds(start, size))]
    return ref.at[(*lead, pl.ds(start, size), slice(None))]


def kernel(dims, arrays, modes, *refs):
    n, e = len(dims), arrays
    xs, ys = refs[:n], refs[n : n + e]
    sums, outs = refs[n + e : 2 * n + e], refs[2 * n + e : 2 * (n + e)]
    scratch = refs[2 * (n + e) :]
    first, held, second = scratch[:n], scratch[n : 2 * n], scratch[2 * n : 3 * n]
    send, recv, dp_send, dp_recv, local_sem = scratch[3 * n :]
    dp, mp = lax.axis_index("dp"), lax.axis_index("mp")
    at = (mp // SIDE, mp % SIDE)

    def peer(axis, k):
        j = (at[axis] + k) % SIDE
        return j, (dp, j * SIDE + at[1] if axis == 0 else at[0] * SIDE + j)

    barrier = pltpu.get_barrier_semaphore()
    greeted = 0
    if n:
        for axis in (0, 1):
            for k in range(1, SIDE):
                pl.semaphore_signal(barrier, inc=1, device_id=peer(axis, k)[1], device_id_type=MESH)
                greeted += 1
    if e:
        for k in range(1, N_DP):
            pl.semaphore_signal(
                barrier, inc=1, device_id=((dp + k) % N_DP, mp), device_id_type=MESH
            )
            greeted += 1
    pl.semaphore_wait(barrier, greeted)

    started = []

    def send_to(src, dst, index, device):
        copy = pltpu.make_async_remote_copy(
            src_ref=src,
            dst_ref=dst,
            send_sem=send.at[index],
            recv_sem=recv.at[index],
            device_id=device,
            device_id_type=MESH,
        )
        copy.start()
        started.append(copy)
        return copy

    todo = [(h, a) for h in range(2) for a in range(n)]
    flight = {}

    def spot(a, h):
        size = xs[a].shape[dims[a]]
        p, q = (1, 0) if h == 0 else (0, 1)
        return p, q, h * (size // 2), size // 8, size // 32

    def index(stage, h, a, k):
        return ((stage * 2 + h) * n + a) * 3 + k - 1

    order = (2, 1, 3)
    for h, a in todo:
        p, q, base, big, small = spot(a, h)
        copies = []
        for k in order:
            j, device = peer(p, k)
            start = pl.multiple_of(base + j * big, big)
            copies.append(
                send_to(
                    cut(xs[a], dims[a], start, big),
                    first[a].at[h, k - 1],
                    index(0, h, a, k),
                    device,
                )
            )
        flight[0, h, a] = copies
    exchanges = []
    for i, mode in enumerate(modes):
        which, block, blocks, split = mode
        rows = ys[which].shape[0] // blocks
        here = pl.ds(pl.multiple_of((block * N_DP + dp) * rows, rows), rows)
        width = outs[which].shape[1]

        def part(to):
            if not split:
                return ys[which].at[pl.ds(block * rows, rows), :]
            return ys[which].at[:, pl.ds(pl.multiple_of(to * width, width), width)]

        landing = outs[which].at[here, :]
        own = pltpu.make_async_copy(part(dp), landing, local_sem.at[i])
        own.start()
        exchanges.append(own)
        for k in (4, 3, 5, 2, 6, 1, 7):
            to = (dp + k) % N_DP
            copy = pltpu.make_async_remote_copy(
                src_ref=part(to),
                dst_ref=landing,
                send_sem=dp_send.at[i * 7 + k - 1],
                recv_sem=dp_recv.at[i * 7 + k - 1],
                device_id=(to, mp),
                device_id_type=MESH,
            )
            copy.start()
            exchanges.append(copy)
    for h, a in todo:
        p, q, base, big, small = spot(a, h)
        for copy in flight[0, h, a]:
            copy.wait_recv()
        start = pl.multiple_of(base + at[p] * big, big)
        total = cut(xs[a], dims[a], start, big)[...].astype(jnp.float32)
        for k in range(3):
            total += first[a][h, k].astype(jnp.float32)
        held[a][h] = total.astype(jnp.bfloat16)
        copies = []
        for k in order:
            j, device = peer(q, k)
            copies.append(
                send_to(
                    cut(held[a], dims[a], pl.multiple_of(j * small, small), small, (h,)),
                    second[a].at[h, k - 1],
                    index(1, h, a, k),
                    device,
                )
            )
        flight[1, h, a] = copies
    for h, a in todo:
        p, q, base, big, small = spot(a, h)
        for copy in flight[1, h, a]:
            copy.wait_recv()
        total = cut(held[a], dims[a], pl.multiple_of(at[q] * small, small), small, (h,))[
            ...
        ].astype(jnp.float32)
        for k in range(3):
            total += second[a][h, k].astype(jnp.float32)
        block = cut(
            sums[a], dims[a], pl.multiple_of(base + at[p] * big + at[q] * small, small), small
        )
        block[...] = total.astype(jnp.bfloat16)
        flight[2, h, a] = [
            send_to(block, block, index(2, h, a, k), peer(q, k)[1]) for k in order
        ]
    for h, a in todo:
        p, q, base, big, small = spot(a, h)
        for copy in flight[2, h, a]:
            copy.wait_recv()
        block = cut(sums[a], dims[a], pl.multiple_of(base + at[p] * big, big), big)
        flight[3, h, a] = [
            send_to(block, block, index(3, h, a, k), peer(p, k)[1]) for k in order
        ]
    for h, a in todo:
        for copy in flight[3, h, a]:
            copy.wait_recv()
    for copy in started:
        copy.wait_send()
    for copy in exchanges:
        copy.wait()


def communicate(number, name, adds=(), moves=()):
    dims = [dim for _, dim in adds]
    modes = []
    for i, (_, mode) in enumerate(moves):
        if mode == "transpose":
            modes.append((i, 0, 1, True))
        else:
            modes.extend((i, s, mode, False) for s in range(mode))
    arrays = [x for x, _ in adds] + [y for y, _ in moves]
    shapes = [x.shape for x, _ in adds]
    for y, mode in moves:
        width = y.shape[1] // N_DP if mode == "transpose" else y.shape[1]
        shapes.append((y.shape[0] * N_DP, width))

    def piece(x, dim, parts):
        shape = list(x.shape)
        shape[dim] //= parts
        return tuple(shape)

    first = [pltpu.VMEM((2, 3, *piece(x, d, 8)), jnp.bfloat16) for x, d in adds]
    held = [pltpu.VMEM((2, *piece(x, d, 8)), jnp.bfloat16) for x, d in adds]
    second = [pltpu.VMEM((2, 3, *piece(x, d, 32)), jnp.bfloat16) for x, d in adds]
    dma = pltpu.SemaphoreType.DMA
    return pl.pallas_call(
        functools.partial(kernel, dims, len(moves), modes),
        out_shape=[jax.ShapeDtypeStruct(s, jnp.bfloat16) for s in shapes],
        in_specs=[pl.BlockSpec(memory_space=pltpu.VMEM)] * len(arrays),
        out_specs=[pl.BlockSpec(memory_space=pltpu.VMEM)] * len(arrays),
        scratch_shapes=[
            *first,
            *held,
            *second,
            dma((max(24 * len(adds), 1),)),
            dma((max(24 * len(adds), 1),)),
            dma((max(7 * len(modes), 1),)),
            dma((max(7 * len(modes), 1),)),
            dma((max(len(modes), 1),)),
        ],
        compiler_params=pltpu.CompilerParams(
            collective_id=number, has_side_effects=True, vmem_limit_bytes=32 * 1024 * 1024
        ),
        name=name,
    )(*arrays)


def mix_kernel(x, out, first, held, second, piece, send, recv, dp_send, dp_recv, local_sem):
    dp, mp = lax.axis_index("dp"), lax.axis_index("mp")
    at = (mp // SIDE, mp % SIDE)
    rows, half = x.shape[0], x.shape[1] // 2
    big, small = rows // 4, rows // 16
    few = small // N_DP
    wide = out.shape[1] // 2

    def peer(axis, k):
        j = (at[axis] + k) % SIDE
        return j, (dp, j * SIDE + at[1] if axis == 0 else at[0] * SIDE + j)

    barrier = pltpu.get_barrier_semaphore()
    for axis in (0, 1):
        for k in range(1, SIDE):
            pl.semaphore_signal(barrier, inc=1, device_id=peer(axis, k)[1], device_id_type=MESH)
    for k in range(1, N_DP):
        pl.semaphore_signal(barrier, inc=1, device_id=((dp + k) % N_DP, mp), device_id_type=MESH)
    pl.semaphore_wait(barrier, 2 * (SIDE - 1) + N_DP - 1)

    started = []

    def send_to(src, dst, sems, index, device):
        copy = pltpu.make_async_remote_copy(
            src_ref=src,
            dst_ref=dst,
            send_sem=sems[0].at[index],
            recv_sem=sems[1].at[index],
            device_id=device,
            device_id_type=MESH,
        )
        copy.start()
        started.append(copy)
        return copy

    over_mp, over_dp = (send, recv), (dp_send, dp_recv)
    order = (2, 1, 3)
    axes = ((1, 0), (0, 1))
    flight = {}

    def index(stage, h, k):
        return (stage * 2 + h) * 3 + k - 1

    for h in range(2):
        p, q = axes[h]
        copies = []
        for k in order:
            j, device = peer(p, k)
            src = x.at[pl.ds(pl.multiple_of(j * big, big), big), pl.ds(h * half, half)]
            copies.append(send_to(src, first.at[h, k - 1], over_mp, index(0, h, k), device))
        flight[0, h] = copies
    for h in range(2):
        p, q = axes[h]
        for copy in flight[0, h]:
            copy.wait_recv()
        total = x[pl.ds(pl.multiple_of(at[p] * big, big), big), pl.ds(h * half, half)].astype(
            jnp.float32
        )
        for k in range(3):
            total += first[h, k].astype(jnp.float32)
        held[h] = total.astype(jnp.bfloat16)
        copies = []
        for k in order:
            j, device = peer(q, k)
            src = held.at[h, pl.ds(pl.multiple_of(j * small, small), small), :]
            copies.append(send_to(src, second.at[h, k - 1], over_mp, index(1, h, k), device))
        flight[1, h] = copies
    for h in range(2):
        p, q = axes[h]
        for copy in flight[1, h]:
            copy.wait_recv()
        total = held[h, pl.ds(pl.multiple_of(at[q] * small, small), small), :].astype(jnp.float32)
        for k in range(3):
            total += second[h, k].astype(jnp.float32)
        piece[h] = total.astype(jnp.bfloat16)
        tokens = pl.ds(pl.multiple_of((at[p] * SIDE + at[q]) * few, few), few)
        landing = out.at[tokens, pl.ds(pl.multiple_of(h * wide + dp * half, half), half)]
        own = pltpu.make_async_copy(
            piece.at[h, pl.ds(pl.multiple_of(dp * few, few), few), :], landing, local_sem.at[h]
        )
        own.start()
        copies = []
        for k in (4, 3, 5, 2, 6, 1, 7):
            to = (dp + k) % N_DP
            src = piece.at[h, pl.ds(pl.multiple_of(to * few, few), few), :]
            copies.append(send_to(src, landing, over_dp, h * 7 + k - 1, (to, mp)))
        flight[2, h] = (own, copies)
    for h in range(2):
        p, q = axes[h]
        own, copies = flight[2, h]
        own.wait()
        for copy in copies:
            copy.wait_recv()
        tokens = pl.ds(pl.multiple_of((at[p] * SIDE + at[q]) * few, few), few)
        block = out.at[tokens, pl.ds(h * wide, wide)]
        flight[3, h] = [
            send_to(block, block, over_mp, index(2, h, k), peer(q, k)[1]) for k in order
        ]
    for h in range(2):
        p, q = axes[h]
        for copy in flight[3, h]:
            copy.wait_recv()
        tokens = pl.ds(pl.multiple_of(at[p] * SIDE * few, SIDE * few), SIDE * few)
        block = out.at[tokens, pl.ds(h * wide, wide)]
        flight[4, h] = [
            send_to(block, block, over_mp, index(3, h, k), peer(p, k)[1]) for k in order
        ]
    for h in range(2):
        for copy in flight[4, h]:
            copy.wait_recv()
    for copy in started:
        copy.wait_send()


def mix(x):
    rows, columns = x.shape
    dma = pltpu.SemaphoreType.DMA
    half = columns // 2
    return pl.pallas_call(
        mix_kernel,
        out_shape=jax.ShapeDtypeStruct((rows // N_DP, columns * N_DP), jnp.bfloat16),
        in_specs=[pl.BlockSpec(memory_space=pltpu.VMEM)],
        out_specs=pl.BlockSpec(memory_space=pltpu.VMEM),
        scratch_shapes=[
            pltpu.VMEM((2, 3, rows // 4, half), jnp.bfloat16),
            pltpu.VMEM((2, rows // 4, half), jnp.bfloat16),
            pltpu.VMEM((2, 3, rows // 16, half), jnp.bfloat16),
            pltpu.VMEM((2, rows // 16, half), jnp.bfloat16),
            dma((24,)),
            dma((24,)),
            dma((14,)),
            dma((14,)),
            dma((2,)),
        ],
        compiler_params=pltpu.CompilerParams(
            collective_id=0, has_side_effects=True, vmem_limit_bytes=32 * 1024 * 1024
        ),
        name="sum_mixed",
    )(x)


def contract_cols(left, right):
    return lax.dot_general(
        left, right, (((1,), (1,)), ((), ())), preferred_element_type=jnp.float32
    )


def contract_rows(left, right):
    return lax.dot_general(
        left, right, (((0,), (0,)), ((), ())), preferred_element_type=jnp.float32
    )


def local(acts, w_up, out_grad, rotation):
    inv_root = D ** (-0.5)
    rows = acts.shape[0]
    me = lax.axis_index("dp")
    tokens = rows * lax.axis_size("dp")
    rot_half = rotation.astype(jnp.bfloat16)
    rot_rows = lax.all_gather(rot_half, "dp", axis=1, tiled=True)
    (acts_all,) = communicate(5, "gather_acts", [], [(acts, 1)])
    blocks = SIDE * SIDE
    by_block = acts_all.reshape(-1, blocks, rows // blocks, acts.shape[1])
    by_block = by_block.transpose(1, 0, 2, 3).reshape(acts_all.shape)
    mixed_part = (
        jnp.dot(by_block, rot_half, preferred_element_type=jnp.float32) * inv_root
    ).astype(jnp.bfloat16)
    mixed = mix(mixed_part)
    run = mixed.shape[1] // (2 * N_DP)
    starts = [(h * N_DP + d) * run for d in range(N_DP) for h in range(2)]
    mixed = jnp.concatenate([mixed[:, start : start + run] for start in starts], axis=1)
    hidden = jnp.dot(mixed, w_up, preferred_element_type=jnp.float32)
    sigmoid_hidden = jax.nn.sigmoid(hidden)
    grad_hidden = (
        out_grad.astype(jnp.float32) * sigmoid_hidden * (1.0 + hidden * (1.0 - sigmoid_hidden))
    ).astype(jnp.bfloat16)
    grad_hidden = lax.optimization_barrier(grad_hidden)
    grad_part = contract_cols(grad_hidden, w_up).astype(jnp.bfloat16)
    grad_mixed, right = communicate(1, "sum_grad", [(grad_part, 1)], [(mixed, "transpose")])
    factor = contract_cols(grad_mixed, rot_rows).astype(jnp.bfloat16)
    (factor_all,) = communicate(2, "gather_factor", [], [(factor, 1)])
    spread_rows = jnp.concatenate((factor_all, acts_all), axis=0)
    skew_rows = jnp.concatenate((acts_all, -factor_all), axis=0)
    own = jnp.concatenate((acts, -factor), axis=0)
    left_part = (
        jnp.dot(factor_all, rot_half, preferred_element_type=jnp.float32) * inv_root
    ).astype(jnp.bfloat16)
    gram_part = contract_cols(spread_rows, own).astype(jnp.bfloat16)
    (gram,) = communicate(3, "sum_gram", [(gram_part, 0)], [])
    second = contract_rows(gram, skew_rows).astype(jnp.bfloat16)
    eye = jnp.eye(rows, dtype=jnp.float32)
    act_sq = lax.dynamic_slice(gram, (tokens + me * rows, 0), (rows, rows))
    factor_sq = lax.dynamic_slice(gram, (me * rows, rows), (rows, rows))
    squares = jnp.concatenate(
        (jnp.sum(act_sq * eye, axis=0), jnp.sum(factor_sq * -eye, axis=0))
    ).astype(jnp.bfloat16)
    squares = jnp.broadcast_to(squares, (16, 2 * rows))
    left, second_all, parts = communicate(
        4, "sum_left", [(left_part, 0)], [(second, 2), (squares, 1)]
    )
    parts = parts[::16].astype(jnp.float32)
    act_norm = jnp.sum(parts[:, :rows])
    factor_norm = jnp.sum(parts[:, rows:])
    spread = (tokens ** (-0.5) + D ** (-0.5)) ** 2
    step_size = (
        step_gain
        * math.sqrt(D)
        / (jnp.sqrt((act_norm + epsilon) * (factor_norm + epsilon)) * spread)
    )
    second_map = (
        skew_rows.astype(jnp.float32) - (step_size * inv_root) * second_all.astype(jnp.float32)
    ).astype(jnp.bfloat16)
    sides = jnp.concatenate((left, right), axis=0)
    half = rotation - (2 * step_size) * contract_rows(skew_rows, sides)
    full = rotation - (2 * step_size) * contract_rows(second_map, sides)
    return half, full


def solution(mesh):
    placed = (P("dp", "mp"), P(None, "mp"), P("dp", "mp"), P("mp", "dp"))
    return jax.shard_map(
        local,
        mesh=mesh,
        in_specs=placed,
        out_specs=(P("mp", "dp"), P("mp", "dp")),
        check_vma=False,
    )
```

```python
import functools
import math

import jax
import jax.numpy as jnp
from jax import lax
from jax.experimental import pallas as pl
from jax.experimental.pallas import tpu as pltpu
from jax.sharding import PartitionSpec as P

D = 8192
step_gain = 0.5
epsilon = 1e-06


MESH = pl.DeviceIdType.MESH
N_DP = 8
SIDE = 4


def cut(ref, dim, start, size, lead=()):
    if dim == 1:
        return ref.at[(*lead, slice(None), pl.ds(start, size))]
    return ref.at[(*lead, pl.ds(start, size), slice(None))]


def kernel(dims, arrays, modes, *refs):
    n, e = len(dims), arrays
    xs, ys = refs[:n], refs[n : n + e]
    sums, outs = refs[n + e : 2 * n + e], refs[2 * n + e : 2 * (n + e)]
    scratch = refs[2 * (n + e) :]
    first, held, second = scratch[:n], scratch[n : 2 * n], scratch[2 * n : 3 * n]
    send, recv, dp_send, dp_recv, local_sem = scratch[3 * n :]
    dp, mp = lax.axis_index("dp"), lax.axis_index("mp")
    at = (mp // SIDE, mp % SIDE)

    def peer(axis, k):
        j = (at[axis] + k) % SIDE
        return j, (dp, j * SIDE + at[1] if axis == 0 else at[0] * SIDE + j)

    barrier = pltpu.get_barrier_semaphore()
    greeted = 0
    if n:
        for axis in (0, 1):
            for k in range(1, SIDE):
                pl.semaphore_signal(barrier, inc=1, device_id=peer(axis, k)[1], device_id_type=MESH)
                greeted += 1
    if e:
        for k in range(1, N_DP):
            pl.semaphore_signal(
                barrier, inc=1, device_id=((dp + k) % N_DP, mp), device_id_type=MESH
            )
            greeted += 1
    pl.semaphore_wait(barrier, greeted)

    started = []

    def send_to(src, dst, index, device):
        copy = pltpu.make_async_remote_copy(
            src_ref=src,
            dst_ref=dst,
            send_sem=send.at[index],
            recv_sem=recv.at[index],
            device_id=device,
            device_id_type=MESH,
        )
        copy.start()
        started.append(copy)
        return copy

    todo = [(h, a) for h in range(2) for a in range(n)]
    flight = {}

    def spot(a, h):
        size = xs[a].shape[dims[a]]
        p, q = (1, 0) if h == 0 else (0, 1)
        return p, q, h * (size // 2), size // 8, size // 32

    def index(stage, h, a, k):
        return ((stage * 2 + h) * n + a) * 3 + k - 1

    order = (2, 1, 3)
    for h, a in todo:
        p, q, base, big, small = spot(a, h)
        copies = []
        for k in order:
            j, device = peer(p, k)
            start = pl.multiple_of(base + j * big, big)
            copies.append(
                send_to(
                    cut(xs[a], dims[a], start, big),
                    first[a].at[h, k - 1],
                    index(0, h, a, k),
                    device,
                )
            )
        flight[0, h, a] = copies
    exchanges, relays = [], []
    partner = dp + 1 - 2 * (dp % 2)
    for i, mode in enumerate(modes):
        which, block, blocks, split = mode
        rows = ys[which].shape[0] // blocks
        here = pl.ds(pl.multiple_of((block * N_DP + dp) * rows, rows), rows)
        width = outs[which].shape[1]

        def part(to):
            if not split:
                return ys[which].at[pl.ds(block * rows, rows), :]
            return ys[which].at[:, pl.ds(pl.multiple_of(to * width, width), width)]

        landing = outs[which].at[here, :]
        own = pltpu.make_async_copy(part(dp), landing, local_sem.at[i])
        own.start()
        exchanges.append(own)
        for k in (4, 3, 5, 2, 6, 1, 7) if split else (4, 2, 6, 1):
            to = (dp + k) % N_DP if k > 1 or split else partner
            copy = pltpu.make_async_remote_copy(
                src_ref=part(to),
                dst_ref=landing,
                send_sem=dp_send.at[i * 7 + k - 1],
                recv_sem=dp_recv.at[i * 7 + k - 1],
                device_id=(to, mp),
                device_id_type=MESH,
            )
            copy.start()
            if split or k == 1:
                exchanges.append(copy)
            else:
                relays.append((i, k, copy))
    for h, a in todo:
        p, q, base, big, small = spot(a, h)
        for copy in flight[0, h, a]:
            copy.wait_recv()
        start = pl.multiple_of(base + at[p] * big, big)
        total = cut(xs[a], dims[a], start, big)[...].astype(jnp.float32)
        for k in range(3):
            total += first[a][h, k].astype(jnp.float32)
        held[a][h] = total.astype(jnp.bfloat16)
        copies = []
        for k in order:
            j, device = peer(q, k)
            copies.append(
                send_to(
                    cut(held[a], dims[a], pl.multiple_of(j * small, small), small, (h,)),
                    second[a].at[h, k - 1],
                    index(1, h, a, k),
                    device,
                )
            )
        flight[1, h, a] = copies
    for h, a in todo:
        p, q, base, big, small = spot(a, h)
        for copy in flight[1, h, a]:
            copy.wait_recv()
        total = cut(held[a], dims[a], pl.multiple_of(at[q] * small, small), small, (h,))[
            ...
        ].astype(jnp.float32)
        for k in range(3):
            total += second[a][h, k].astype(jnp.float32)
        block = cut(
            sums[a], dims[a], pl.multiple_of(base + at[p] * big + at[q] * small, small), small
        )
        block[...] = total.astype(jnp.bfloat16)
        flight[2, h, a] = [
            send_to(block, block, index(2, h, a, k), peer(q, k)[1]) for k in order
        ]
    for h, a in todo:
        p, q, base, big, small = spot(a, h)
        for copy in flight[2, h, a]:
            copy.wait_recv()
        block = cut(sums[a], dims[a], pl.multiple_of(base + at[p] * big, big), big)
        flight[3, h, a] = [
            send_to(block, block, index(3, h, a, k), peer(p, k)[1]) for k in order
        ]
    for i, k, copy in relays:
        copy.wait()
        which, block, blocks, split = modes[i]
        rows = ys[which].shape[0] // blocks
        origin = (dp + N_DP - k) % N_DP
        there = outs[which].at[pl.ds(pl.multiple_of((block * N_DP + origin) * rows, rows), rows), :]
        onward = pltpu.make_async_remote_copy(
            src_ref=there,
            dst_ref=there,
            send_sem=dp_send.at[i * 7 + k],
            recv_sem=dp_recv.at[i * 7 + k],
            device_id=(partner, mp),
            device_id_type=MESH,
        )
        onward.start()
        exchanges.append(onward)
    for h, a in todo:
        for copy in flight[3, h, a]:
            copy.wait_recv()
    for copy in started:
        copy.wait_send()
    for copy in exchanges:
        copy.wait()


def communicate(number, name, adds=(), moves=()):
    dims = [dim for _, dim in adds]
    modes = []
    for i, (_, mode) in enumerate(moves):
        if mode == "transpose":
            modes.append((i, 0, 1, True))
        else:
            modes.extend((i, s, mode, False) for s in range(mode))
    arrays = [x for x, _ in adds] + [y for y, _ in moves]
    shapes = [x.shape for x, _ in adds]
    for y, mode in moves:
        width = y.shape[1] // N_DP if mode == "transpose" else y.shape[1]
        shapes.append((y.shape[0] * N_DP, width))

    def piece(x, dim, parts):
        shape = list(x.shape)
        shape[dim] //= parts
        return tuple(shape)

    first = [pltpu.VMEM((2, 3, *piece(x, d, 8)), jnp.bfloat16) for x, d in adds]
    held = [pltpu.VMEM((2, *piece(x, d, 8)), jnp.bfloat16) for x, d in adds]
    second = [pltpu.VMEM((2, 3, *piece(x, d, 32)), jnp.bfloat16) for x, d in adds]
    dma = pltpu.SemaphoreType.DMA
    return pl.pallas_call(
        functools.partial(kernel, dims, len(moves), modes),
        out_shape=[jax.ShapeDtypeStruct(s, jnp.bfloat16) for s in shapes],
        in_specs=[pl.BlockSpec(memory_space=pltpu.VMEM)] * len(arrays),
        out_specs=[pl.BlockSpec(memory_space=pltpu.VMEM)] * len(arrays),
        scratch_shapes=[
            *first,
            *held,
            *second,
            dma((max(24 * len(adds), 1),)),
            dma((max(24 * len(adds), 1),)),
            dma((max(7 * len(modes), 1),)),
            dma((max(7 * len(modes), 1),)),
            dma((max(len(modes), 1),)),
        ],
        compiler_params=pltpu.CompilerParams(
            collective_id=number, has_side_effects=True, vmem_limit_bytes=32 * 1024 * 1024
        ),
        name=name,
    )(*arrays)


def mix_kernel(x, out, first, held, second, piece, send, recv, dp_send, dp_recv, local_sem):
    dp, mp = lax.axis_index("dp"), lax.axis_index("mp")
    at = (mp // SIDE, mp % SIDE)
    rows, half = x.shape[0], x.shape[1] // 2
    big, small = rows // 4, rows // 16
    few = small // N_DP
    wide = out.shape[1] // 2

    def peer(axis, k):
        j = (at[axis] + k) % SIDE
        return j, (dp, j * SIDE + at[1] if axis == 0 else at[0] * SIDE + j)

    barrier = pltpu.get_barrier_semaphore()
    for axis in (0, 1):
        for k in range(1, SIDE):
            pl.semaphore_signal(barrier, inc=1, device_id=peer(axis, k)[1], device_id_type=MESH)
    for k in range(1, N_DP):
        pl.semaphore_signal(barrier, inc=1, device_id=((dp + k) % N_DP, mp), device_id_type=MESH)
    pl.semaphore_wait(barrier, 2 * (SIDE - 1) + N_DP - 1)

    started = []

    def send_to(src, dst, sems, index, device):
        copy = pltpu.make_async_remote_copy(
            src_ref=src,
            dst_ref=dst,
            send_sem=sems[0].at[index],
            recv_sem=sems[1].at[index],
            device_id=device,
            device_id_type=MESH,
        )
        copy.start()
        started.append(copy)
        return copy

    over_mp, over_dp = (send, recv), (dp_send, dp_recv)
    order = (2, 1, 3)
    axes = ((1, 0), (0, 1))
    flight = {}

    def index(stage, h, k):
        return (stage * 2 + h) * 3 + k - 1

    for h in range(2):
        p, q = axes[h]
        copies = []
        for k in order:
            j, device = peer(p, k)
            src = x.at[pl.ds(pl.multiple_of(j * big, big), big), pl.ds(h * half, half)]
            copies.append(send_to(src, first.at[h, k - 1], over_mp, index(0, h, k), device))
        flight[0, h] = copies
    for h in range(2):
        p, q = axes[h]
        for copy in flight[0, h]:
            copy.wait_recv()
        total = x[pl.ds(pl.multiple_of(at[p] * big, big), big), pl.ds(h * half, half)].astype(
            jnp.float32
        )
        for k in range(3):
            total += first[h, k].astype(jnp.float32)
        held[h] = total.astype(jnp.bfloat16)
        copies = []
        for k in order:
            j, device = peer(q, k)
            src = held.at[h, pl.ds(pl.multiple_of(j * small, small), small), :]
            copies.append(send_to(src, second.at[h, k - 1], over_mp, index(1, h, k), device))
        flight[1, h] = copies
    for h in range(2):
        p, q = axes[h]
        for copy in flight[1, h]:
            copy.wait_recv()
        total = held[h, pl.ds(pl.multiple_of(at[q] * small, small), small), :].astype(jnp.float32)
        for k in range(3):
            total += second[h, k].astype(jnp.float32)
        piece[h] = total.astype(jnp.bfloat16)
        tokens = pl.ds(pl.multiple_of((at[p] * SIDE + at[q]) * few, few), few)
        landing = out.at[tokens, pl.ds(pl.multiple_of(h * wide + dp * half, half), half)]
        own = pltpu.make_async_copy(
            piece.at[h, pl.ds(pl.multiple_of(dp * few, few), few), :], landing, local_sem.at[h]
        )
        own.start()
        copies = []
        for k in (4, 3, 5, 2, 6, 1, 7):
            to = (dp + k) % N_DP
            src = piece.at[h, pl.ds(pl.multiple_of(to * few, few), few), :]
            copies.append(send_to(src, landing, over_dp, h * 7 + k - 1, (to, mp)))
        flight[2, h] = (own, copies)
    for h in range(2):
        p, q = axes[h]
        own, copies = flight[2, h]
        own.wait()
        for copy in copies:
            copy.wait_recv()
        tokens = pl.ds(pl.multiple_of((at[p] * SIDE + at[q]) * few, few), few)
        block = out.at[tokens, pl.ds(h * wide, wide)]
        flight[3, h] = [
            send_to(block, block, over_mp, index(2, h, k), peer(q, k)[1]) for k in order
        ]
    for h in range(2):
        p, q = axes[h]
        for copy in flight[3, h]:
            copy.wait_recv()
        tokens = pl.ds(pl.multiple_of(at[p] * SIDE * few, SIDE * few), SIDE * few)
        block = out.at[tokens, pl.ds(h * wide, wide)]
        flight[4, h] = [
            send_to(block, block, over_mp, index(3, h, k), peer(p, k)[1]) for k in order
        ]
    for h in range(2):
        for copy in flight[4, h]:
            copy.wait_recv()
    for copy in started:
        copy.wait_send()


def mix(x):
    rows, columns = x.shape
    dma = pltpu.SemaphoreType.DMA
    half = columns // 2
    return pl.pallas_call(
        mix_kernel,
        out_shape=jax.ShapeDtypeStruct((rows // N_DP, columns * N_DP), jnp.bfloat16),
        in_specs=[pl.BlockSpec(memory_space=pltpu.VMEM)],
        out_specs=pl.BlockSpec(memory_space=pltpu.VMEM),
        scratch_shapes=[
            pltpu.VMEM((2, 3, rows // 4, half), jnp.bfloat16),
            pltpu.VMEM((2, rows // 4, half), jnp.bfloat16),
            pltpu.VMEM((2, 3, rows // 16, half), jnp.bfloat16),
            pltpu.VMEM((2, rows // 16, half), jnp.bfloat16),
            dma((24,)),
            dma((24,)),
            dma((14,)),
            dma((14,)),
            dma((2,)),
        ],
        compiler_params=pltpu.CompilerParams(
            collective_id=0, has_side_effects=True, vmem_limit_bytes=32 * 1024 * 1024
        ),
        name="sum_mixed",
    )(x)


def contract_cols(left, right):
    return lax.dot_general(
        left, right, (((1,), (1,)), ((), ())), preferred_element_type=jnp.float32
    )


def contract_rows(left, right):
    return lax.dot_general(
        left, right, (((0,), (0,)), ((), ())), preferred_element_type=jnp.float32
    )


def local(acts, w_up, out_grad, rotation):
    inv_root = D ** (-0.5)
    rows = acts.shape[0]
    me = lax.axis_index("dp")
    tokens = rows * lax.axis_size("dp")
    rot_half = rotation.astype(jnp.bfloat16)
    rot_rows = lax.all_gather(rot_half, "dp", axis=1, tiled=True)
    (acts_all,) = communicate(5, "gather_acts", [], [(acts, 1)])
    blocks = SIDE * SIDE
    by_block = acts_all.reshape(-1, blocks, rows // blocks, acts.shape[1])
    by_block = by_block.transpose(1, 0, 2, 3).reshape(acts_all.shape)
    mixed_part = (
        jnp.dot(by_block, rot_half, preferred_element_type=jnp.float32) * inv_root
    ).astype(jnp.bfloat16)
    mixed = mix(mixed_part)
    run = mixed.shape[1] // (2 * N_DP)
    starts = [(h * N_DP + d) * run for d in range(N_DP) for h in range(2)]
    mixed = jnp.concatenate([mixed[:, start : start + run] for start in starts], axis=1)
    hidden = jnp.dot(mixed, w_up, preferred_element_type=jnp.float32)
    sigmoid_hidden = jax.nn.sigmoid(hidden)
    grad_hidden = (
        out_grad.astype(jnp.float32) * sigmoid_hidden * (1.0 + hidden * (1.0 - sigmoid_hidden))
    ).astype(jnp.bfloat16)
    grad_hidden = lax.optimization_barrier(grad_hidden)
    grad_part = contract_cols(grad_hidden, w_up).astype(jnp.bfloat16)
    grad_mixed, right = communicate(1, "sum_grad", [(grad_part, 1)], [(mixed, "transpose")])
    factor = contract_cols(grad_mixed, rot_rows).astype(jnp.bfloat16)
    (factor_all,) = communicate(2, "gather_factor", [], [(factor, 1)])
    spread_rows = jnp.concatenate((factor_all, acts_all), axis=0)
    skew_rows = jnp.concatenate((acts_all, -factor_all), axis=0)
    own = jnp.concatenate((acts, -factor), axis=0)
    left_part = (
        jnp.dot(factor_all, rot_half, preferred_element_type=jnp.float32) * inv_root
    ).astype(jnp.bfloat16)
    gram_part = contract_cols(spread_rows, own).astype(jnp.bfloat16)
    (gram,) = communicate(3, "sum_gram", [(gram_part, 0)], [])
    second = contract_rows(gram, skew_rows).astype(jnp.bfloat16)
    eye = jnp.eye(rows, dtype=jnp.float32)
    act_sq = lax.dynamic_slice(gram, (tokens + me * rows, 0), (rows, rows))
    factor_sq = lax.dynamic_slice(gram, (me * rows, rows), (rows, rows))
    squares = jnp.concatenate(
        (jnp.sum(act_sq * eye, axis=0), jnp.sum(factor_sq * -eye, axis=0))
    ).astype(jnp.bfloat16)
    squares = jnp.broadcast_to(squares, (16, 2 * rows))
    left, second_all, parts = communicate(
        4, "sum_left", [(left_part, 0)], [(second, 2), (squares, 1)]
    )
    parts = parts[::16].astype(jnp.float32)
    act_norm = jnp.sum(parts[:, :rows])
    factor_norm = jnp.sum(parts[:, rows:])
    spread = (tokens ** (-0.5) + D ** (-0.5)) ** 2
    step_size = (
        step_gain
        * math.sqrt(D)
        / (jnp.sqrt((act_norm + epsilon) * (factor_norm + epsilon)) * spread)
    )
    second_map = (
        skew_rows.astype(jnp.float32) - (step_size * inv_root) * second_all.astype(jnp.float32)
    ).astype(jnp.bfloat16)
    sides = jnp.concatenate((left, right), axis=0)
    half = rotation - (2 * step_size) * contract_rows(skew_rows, sides)
    full = rotation - (2 * step_size) * contract_rows(second_map, sides)
    return half, full


def solution(mesh):
    placed = (P("dp", "mp"), P(None, "mp"), P("dp", "mp"), P("mp", "dp"))
    return jax.shard_map(
        local,
        mesh=mesh,
        in_specs=placed,
        out_specs=(P("mp", "dp"), P("mp", "dp")),
        check_vma=False,
    )
```
